512 devices in a mesh: seq: 16 (over x, y_hi, core), head: 32 (over z, y_lo).
Axes of the slice: x: 4, y: 4 (y_hi: 2, y_lo: 2; y = y_hi * 2 + y_lo), z: 16, core: 2. Of those that a mesh axis runs over, the one named last changes fastest.
Arguments:
- x_inner: bfloat16 [24576, 16384], P('seq', 'head'), may hold values from -400 to 400
- z_gate: bfloat16 [24576, 16384], P('seq', 'head'), may hold values from -6 to 6
- bc_raw: bfloat16 [24576, 512], P(('seq', 'head')), may hold values from -6 to 6
- conv_weight: float32 [4, 512], replicated, may hold values from -3 to 3
- conv_bias: float32 [512], replicated, may hold values from -3 to 3
- dt_raw: float32 [24576, 128], P('seq', 'head'), may hold values from -6 to 24576
- a_log: float32 [128], P('head'), may hold values from -20 to 1
- d_skip: float32 [128], P('head'), may hold values from 0.5 to 1.5
- norm_gain: float32 [16384], P('head'), may hold values from 0.5 to 1.5
Outputs:
- mixer_out: bfloat16 [24576, 16384], P('seq', 'head')
The draws below stay inside these ranges and needn't reach their ends.
All inputs are finite; a program needn't handle non-finite values.
Results may differ from the reference program's by a relative error of at most 0.0034.
Values may be sent and summed in bfloat16 or wider, within the bound.
A program may use at most 64 MiB of HBM per device.

```python
import math
import jax
import jax.numpy as jnp
from jax import lax

HEADS = 128
HEAD_DIM = 128
STATE = 256
CONV = 4
BLOCK = 256
SEQ_DEV = 1536
TOKENS = 24576
INNER = 16384


def decay_rates(key):
    subkeys = jax.random.split(jax.random.fold_in(key, 7), 6)
    quick_share = 0.5
    fast_flags = jax.random.uniform(subkeys[0], (HEADS,)) < quick_share
    jitter = jax.random.uniform(subkeys[1], (HEADS,), minval=-0.15, maxval=0.15)
    slow_rate = 0.3 / (TOKENS * 0.05)
    velocity_values = jnp.where(fast_flags, 0.5, slow_rate) * jnp.exp(jitter)
    roughness = jax.random.uniform(subkeys[2], (TOKENS, HEADS), minval=0.5, maxval=1.5)
    blocks = jnp.exp(jax.random.uniform(subkeys[3], (TOKENS // SEQ_DEV, HEADS), minval=-0.7, maxval=0.7))
    delta_widths = 0.05 * roughness * jnp.repeat(blocks, SEQ_DEV, axis=0)
    places = jax.random.randint(subkeys[4], (HEADS, 3), 0, TOKENS)
    penalty_terms = jax.random.uniform(subkeys[5], (HEADS, 3), minval=0.22, maxval=0.51)
    agreement_flags = (jnp.arange(TOKENS)[:, None, None] == places[None]).astype(jnp.float32)
    spike_penalty = jnp.sum(agreement_flags * penalty_terms[None], axis=2)
    flagged_entries = (spike_penalty > 0.0) & jnp.logical_not(fast_flags)[None, :]
    delta_widths = jnp.where(flagged_entries, spike_penalty / velocity_values[None, :], delta_widths)
    return (velocity_values, delta_widths, flagged_entries)


def draw_a_log(key, part):
    velocity_values, delta_widths, flagged_entries = decay_rates(key)
    return jnp.log(velocity_values).astype(jnp.float32)


def draw_dt_raw(key, part):
    velocity_values, delta_widths, flagged_entries = decay_rates(key)
    return (delta_widths + jnp.log(-jnp.expm1(-delta_widths))).astype(jnp.float32)


def draw_x_inner(key, part):
    velocity_values, delta_widths, flagged_entries = decay_rates(key)
    subkeys = jax.random.split(jax.random.fold_in(key, 11), 3)
    values = jnp.clip(jax.random.normal(subkeys[0], (TOKENS, INNER), jnp.float32), -4.0, 4.0)
    channel_scale = jnp.exp(jax.random.uniform(subkeys[1], (INNER,), minval=0.0, maxval=math.log(10.0)))
    token_scale = jnp.exp(jax.random.uniform(subkeys[2], (TOKENS, 1), minval=0.0, maxval=math.log(10.0)))
    rise_base = 3.0
    head_rise = rise_base ** ((jnp.arange(INNER) // HEAD_DIM).astype(jnp.float32) / HEADS)
    damping = jnp.repeat(jnp.where(flagged_entries, 0.05 / delta_widths, 1.0), HEAD_DIM, axis=1)
    return (values * channel_scale[None, :] * head_rise[None, :] * token_scale * damping / 10.0).astype(jnp.bfloat16)


def level_of(key, extent, shards, low, high):
    gain = 1.0
    for dim, blocks in shards:
        draws = jax.random.uniform(jax.random.fold_in(jax.random.fold_in(key, 6), dim), (blocks,), jnp.float32, low / len(shards), high / len(shards))
        gain = gain * jnp.repeat(jnp.exp(draws), extent[dim] // blocks).reshape((-1,) + (1,) * (len(extent) - 1 - dim))
    return gain


def noise(own_key, extent, scale, most, pieces=(), kind=jnp.bfloat16):
    array = jax.random.normal(own_key, extent, jnp.float32) * scale
    if len(pieces) > 0:
        array = level_of(own_key, extent, pieces, -0.22, 0.18) * array
    return jnp.clip(array, min=-most, max=most).astype(kind)


def setup_inputs(seed: int = 0) -> dict:
    keys = jax.random.split(jax.random.key(seed), 10)
    x_inner = draw_x_inner(jax.random.fold_in(keys[9], 71), 0)
    z_gate = noise(keys[1], (TOKENS, INNER), 1.0, 6.0, ((0, 16), (1, 32)))
    bc_raw = noise(keys[2], (TOKENS, 2 * STATE), 1.0, 6.0, ((0, 512),))
    conv_weight = noise(keys[3], (CONV, 2 * STATE), CONV ** -0.5, 3.0, (), jnp.float32)
    conv_bias = noise(keys[4], (2 * STATE,), 0.5, 3.0, (), jnp.float32)
    dt_raw = draw_dt_raw(jax.random.fold_in(keys[9], 71), 0)
    a_log = draw_a_log(jax.random.fold_in(keys[9], 71), 0)
    d_skip = jnp.clip(0.5 + 1.0 * jax.random.uniform(keys[7], (HEADS,), jnp.float32) ** level_of(keys[7], (HEADS,), ((0, 32),), -0.2, 0.2), 0.5, 1.5)
    norm_gain = jnp.clip(1.0 + 0.1 * jax.random.normal(keys[8], (INNER,), jnp.float32), 0.5, 1.5)
    return dict(x_inner=x_inner, z_gate=z_gate, bc_raw=bc_raw, conv_weight=conv_weight, conv_bias=conv_bias, dt_raw=dt_raw, a_log=a_log, d_skip=d_skip, norm_gain=norm_gain)


def convolve_rows(bc_raw, conv_weight, conv_bias):
    tap_count = conv_weight.shape[0]
    row_count = bc_raw.shape[0]
    padded = jnp.concatenate([jnp.zeros((tap_count - 1, bc_raw.shape[1]), jnp.float32), bc_raw.astype(jnp.float32)], axis=0)
    accumulated = jnp.broadcast_to(conv_bias[None, :], (row_count, bc_raw.shape[1]))
    for offset in range(tap_count):
        accumulated = accumulated + conv_weight[offset][None, :] * padded[offset:offset + row_count]
    return jax.nn.silu(accumulated).astype(jnp.bfloat16)

def reference(x_inner, z_gate, bc_raw, conv_weight, conv_bias, dt_raw, a_log, d_skip, norm_gain):
    bc_act = convolve_rows(bc_raw, conv_weight, conv_bias)
    step_size = jax.nn.softplus(dt_raw)
    log_step = -jnp.exp(a_log)[None, :] * step_size
    block_count = TOKENS // BLOCK
    inputs = (x_inner.reshape(block_count, BLOCK, HEADS, HEAD_DIM), z_gate.reshape(block_count, BLOCK, INNER), bc_act.reshape(block_count, BLOCK, 2 * STATE), log_step.reshape(block_count, BLOCK, HEADS), step_size.reshape(block_count, BLOCK, HEADS))
    lower_mask = jnp.tril(jnp.ones((BLOCK, BLOCK), dtype=bool))
    highest = lax.Precision.HIGHEST

    def advance(carried, block_inputs):
        x_block, z_block, bc_block, log_block, size_block = block_inputs
        b_float = bc_block[:, :STATE].astype(jnp.float32)
        c_float = bc_block[:, STATE:].astype(jnp.float32)
        cum_log = jnp.cumsum(log_block, axis=0)
        gram_matrix = jnp.dot(bc_block[:, STATE:], bc_block[:, :STATE].T, preferred_element_type=jnp.float32)
        by_head = cum_log.T
        spread = by_head[:, :, None] - by_head[:, None, :]
        decay_blocks = jnp.where(lower_mask[None], jnp.exp(jnp.where(lower_mask[None], spread, 0.0)), 0.0)
        weights = gram_matrix[None] * decay_blocks * size_block.T[:, None, :]
        x_float = x_block.astype(jnp.float32)
        inner_part = jnp.einsum('hij,jhp->ihp', weights, x_float, precision=highest)
        carried_part = jnp.exp(cum_log)[:, :, None] * jnp.einsum('in,hpn->ihp', c_float, carried, precision=highest)
        tail_weight = jnp.exp(cum_log[-1][None, :] - cum_log) * size_block
        updated = jnp.exp(cum_log[-1])[:, None, None] * carried + jnp.einsum('jhp,jn->hpn', x_float * tail_weight[:, :, None], b_float, precision=highest)
        ssm_out = inner_part + carried_part + d_skip[None, :, None] * x_float
        gated_out = ssm_out.reshape(BLOCK, INNER) * jax.nn.silu(z_block.astype(jnp.float32))
        inverse_rms = lax.rsqrt(lax.optimization_barrier(jnp.sum(gated_out * gated_out, axis=1, keepdims=True)) / INNER + 1e-05)
        return (updated, (gated_out * inverse_rms * norm_gain[None, :]).astype(jnp.bfloat16))
    initial = jnp.zeros((HEADS, HEAD_DIM, STATE), jnp.float32)
    final_state, blocks = lax.scan(advance, initial, inputs)
    return blocks.reshape(TOKENS, INNER)
```

```python
import jax
import jax.numpy as jnp
from jax import lax
from jax.experimental import pallas as pl
from jax.experimental.pallas import tpu as pltpu
from jax.sharding import PartitionSpec as P

HEAD_DIM = 128
STATE = 256
BLOCK = 256
INNER = 16384
NSEQ = 16
NZ = 16
VMEM_SPEC = pl.BlockSpec(memory_space=pltpu.VMEM)
SMEM_SPEC = pl.BlockSpec(memory_space=pltpu.SMEM)
F32 = jnp.float32
BF16 = jnp.bfloat16


def remote(src, dst, send, recv, **where):
    return pltpu.make_async_remote_copy(
        src_ref=src,
        dst_ref=dst,
        send_sem=send,
        recv_sem=recv,
        device_id=where,
        device_id_type=pl.DeviceIdType.MESH,
    )


def greet(targets):
    barrier = pltpu.get_barrier_semaphore()
    for where in targets:
        pl.semaphore_signal(
            barrier, inc=1, device_id=where, device_id_type=pl.DeviceIdType.MESH
        )
    pl.semaphore_wait(barrier, len(targets))


def gather_kernel(raw, out, rim, zsend, zrecv, ysend, yrecv, tsend, trecv, lsem, rsend, rrecv):
    seq = lax.axis_index("seq")
    head = lax.axis_index("head")
    z = head // 2
    yl = head % 2
    right = ((z + 1) % NZ) * 2 + yl
    left = ((z + NZ - 1) % NZ) * 2 + yl
    mate = z * 2 + 1 - yl
    after = (seq + 1) % NSEQ
    before = (seq + NSEQ - 1) % NSEQ
    greet([{"head": right}, {"head": left}, {"head": mate}, {"seq": after}, {"seq": before}])
    sides = (right, left)

    def window(turn):
        return pl.multiple_of(32 * yl + 16 * (turn + yl * (3 - 2 * turn)), 16)

    def span(start, size):
        return pl.ds(pl.multiple_of(start, 16), size)

    def ring(side, step, turn, slot, src):
        return remote(
            src,
            out.at[slot, span(window(turn), 16)],
            zsend.at[side, step, turn],
            zrecv.at[side, step, turn],
            head=sides[side],
        )

    def across(index, slot, src):
        return remote(
            src,
            out.at[slot, span(64 * yl, 32)],
            ysend.at[index],
            yrecv.at[index],
            head=mate,
        )

    sent = []

    def go(copy):
        copy.start()
        sent.append(copy)

    middle = remote(
        raw.at[span(32 - 32 * yl, 16)],
        out.at[z, span(32 + 16 * yl, 16)],
        tsend,
        trecv,
        head=mate,
    )
    go(middle)
    for turn in range(3):
        for side in range(2):
            go(ring(side, 0, turn, z, raw.at[span(window(turn) - 48 * yl, 16)]))
    go(across(0, z, raw.at[span(16 * yl, 32)]))
    own = pltpu.make_async_copy(raw, out.at[z, span(48 * yl, 48)], lsem)
    own.start()
    remote(
        raw.at[span(32 - 32 * yl, 16)],
        out.at[z, span(48 - 16 * yl, 16)],
        tsend,
        trecv,
        head=mate,
    ).wait_recv()
    for side in range(2):
        go(ring(side, 0, 3, z, out.at[z, span(window(3), 16)]))
    for step in range(1, 9):
        slots = ((z + NZ - step) % NZ, (z + step) % NZ)
        for turn in range(4):
            for side in range(2):
                if step == 8 and side != turn // 2:
                    continue
                slot = slots[side]
                piece = out.at[slot, span(window(turn), 16)]
                ring(side, step - 1, turn, slot, piece).wait_recv()
                if step < 7 or (step == 7 and side == turn // 2):
                    go(ring(side, step, turn, slot, piece))
                if turn == 1:
                    index = step + 8 * side
                    go(across(index, slot, out.at[slot, span(64 * yl, 32)]))
    for index in range(16):
        slot = (z + NZ - index) % NZ if index <= 8 else (z + index - 8) % NZ
        landed = out.at[slot, span(64 * (1 - yl), 32)]
        remote(landed, landed, ysend.at[index], yrecv.at[index], head=mate).wait_recv()
    own.wait()
    edge = remote(out.at[NZ - 1, pl.ds(80, 16)], rim, rsend, rrecv, seq=after)
    edge.start()
    for copy in sent:
        copy.wait_send()
    edge.wait()


def gather(raw):
    rows, width = raw.shape
    return pl.pallas_call(
        gather_kernel,
        out_shape=(
            jax.ShapeDtypeStruct((NZ, 2 * rows, width), raw.dtype),
            jax.ShapeDtypeStruct((16, width), raw.dtype),
        ),
        in_specs=[VMEM_SPEC],
        out_specs=(VMEM_SPEC, VMEM_SPEC),
        scratch_shapes=[
            pltpu.SemaphoreType.DMA((2, 8, 4)),
            pltpu.SemaphoreType.DMA((2, 8, 4)),
            pltpu.SemaphoreType.DMA((16,)),
            pltpu.SemaphoreType.DMA((16,)),
            pltpu.SemaphoreType.DMA,
            pltpu.SemaphoreType.DMA,
            pltpu.SemaphoreType.DMA,
            pltpu.SemaphoreType.DMA,
            pltpu.SemaphoreType.DMA,
        ],
        compiler_params=pltpu.CompilerParams(collective_id=0, has_side_effects=True),
        name="gather_bc",
    )(raw)


def split(value):
    high = value.astype(BF16)
    return high, (value - high.astype(F32)).astype(BF16)


def dot(a, b, ca, cb):
    return lax.dot_general(a, b, (((ca,), (cb,)), ((), ())), preferred_element_type=F32)


def spread_heads(column):
    rows = column.shape[0]
    return jnp.concatenate(
        [jnp.broadcast_to(column[:, h : h + 1], (rows, HEAD_DIM)) for h in range(4)], axis=1
    )


def state_step(x, b_in, cum, offset, state):
    last = cum[:, BLOCK - 1 : BLOCK]
    tail = jnp.exp(jnp.transpose(last - offset))
    weighted = x.astype(F32) * spread_heads(tail)
    high, low = split(weighted)
    decay = spread_heads(jnp.transpose(jnp.exp(jnp.broadcast_to(last, (8, 128)))))[0:1]
    return decay * state + dot(b_in, high, 0, 0) + dot(b_in, low, 0, 0), last


def local_kernel(
    a_log, raw, rim, conv_weight, conv_bias, dt, x, act, cum_out, offset_out, message, padded, state, total
):
    block = pl.program_id(0)

    @pl.when(block == 0)
    def _():
        first = lax.axis_index("seq") == 0
        before = rim[...].astype(F32)[8:16, :]
        padded[0:8, :] = jnp.where(first, 0.0, before)
        state[...] = jnp.zeros_like(state)
        total[...] = jnp.zeros_like(total)

    padded[8 : 8 + BLOCK, :] = raw[...].astype(F32)
    summed = jnp.broadcast_to(conv_bias[...], (BLOCK, 2 * STATE))
    for tap in range(4):
        summed = summed + conv_weight[tap : tap + 1, :] * padded[5 + tap : 5 + tap + BLOCK, :]
    acted = jax.nn.silu(summed).astype(BF16)
    act[...] = acted
    padded[0:8, :] = padded[BLOCK : BLOCK + 8, :]

    sub = lax.broadcasted_iota(jnp.int32, (8, BLOCK), 0)
    rate = jnp.full((8, BLOCK), a_log[0], F32)
    for h in range(1, 4):
        rate = jnp.where(sub == h, a_log[h], rate)
    raw_dt = dt[...]
    size = jnp.maximum(raw_dt, 0.0) + jnp.log1p(jnp.exp(-jnp.abs(raw_dt)))
    log_step = -jnp.exp(rate) * size
    row = lax.broadcasted_iota(jnp.int32, (BLOCK, BLOCK), 0)
    column = lax.broadcasted_iota(jnp.int32, (BLOCK, BLOCK), 1)
    upper = jnp.where(row <= column, 1.0, 0.0).astype(BF16)
    high, rest = log_step.astype(BF16), None
    rest = log_step - high.astype(F32)
    middle, low = split(rest)
    cum = (dot(low, upper, 1, 0) + dot(middle, upper, 1, 0)) + dot(high, upper, 1, 0)
    offset = cum - jnp.log(size)
    cum_out[...] = cum
    offset_out[...] = offset
    fresh, last = state_step(x[...], acted[:, :STATE], cum, offset, state[...])
    state[...] = fresh
    total[...] = total[...] + jnp.broadcast_to(last, (8, 128))

    @pl.when(block == pl.num_programs(0) - 1)
    def _():
        gone = spread_heads(jnp.transpose(jnp.exp(total[...])))[0:8]
        for k in range(NSEQ):
            message[k, 0:16, :] = state[16 * k : 16 * k + 16, :]
            message[k, 16:24, :] = gone


def local_states(raw, rim, conv_weight, conv_bias, dt, a_log, x):
    length, width = x.shape
    blocks = length // BLOCK
    by_row = lambda b: (b, 0)
    by_lane = lambda b: (0, b)
    fixed = lambda b: (0, 0)
    return pl.pallas_call(
        local_kernel,
        grid=(blocks,),
        out_shape=(
            jax.ShapeDtypeStruct((length, 2 * STATE), BF16),
            jax.ShapeDtypeStruct((8, length), F32),
            jax.ShapeDtypeStruct((8, length), F32),
            jax.ShapeDtypeStruct((NSEQ, 24, width), F32),
        ),
        in_specs=[
            SMEM_SPEC,
            pl.BlockSpec((BLOCK, 2 * STATE), by_row),
            pl.BlockSpec((16, 2 * STATE), fixed),
            pl.BlockSpec((4, 2 * STATE), fixed),
            pl.BlockSpec((1, 2 * STATE), fixed),
            pl.BlockSpec((8, BLOCK), by_lane),
            pl.BlockSpec((BLOCK, width), by_row),
        ],
        out_specs=(
            pl.BlockSpec((BLOCK, 2 * STATE), by_row),
            pl.BlockSpec((8, BLOCK), by_lane),
            pl.BlockSpec((8, BLOCK), by_lane),
            pl.BlockSpec((NSEQ, 24, width), lambda b: (0, 0, 0)),
        ),
        scratch_shapes=[
            pltpu.VMEM((BLOCK + 8, 2 * STATE), F32),
            pltpu.VMEM((STATE, width), F32),
            pltpu.VMEM((8, 128), F32),
        ],
        name="local_states",
    )(a_log, raw, rim, conv_weight, conv_bias, dt, x)


def scan_kernel(message, out, landed, prefix, asend, arecv, bsend, brecv):
    me = lax.axis_index("seq")
    others = [(me + hop) % NSEQ for hop in range(1, NSEQ)]
    greet([{"seq": other} for other in others])
    sent = []
    for other in others:
        copy = remote(message.at[other], landed.at[me], asend.at[other], arecv.at[me], seq=other)
        copy.start()
        sent.append(copy)
    landed[me] = message[me]
    for other in others:
        remote(
            landed.at[other], landed.at[other], asend.at[other], arecv.at[other], seq=other
        ).wait_recv()
    state = jnp.zeros(prefix.shape[1:], F32)
    for s in range(NSEQ):
        prefix[s] = state
        if s < NSEQ - 1:
            state = landed[s, 16:17, :] * state + landed[s, 0:16, :]
    for other in others:
        copy = remote(prefix.at[other], out.at[me], bsend.at[other], brecv.at[me], seq=other)
        copy.start()
        sent.append(copy)
    out[me] = prefix[me]
    for other in others:
        remote(
            out.at[other], out.at[other], bsend.at[other], brecv.at[other], seq=other
        ).wait_recv()
    for copy in sent:
        copy.wait_send()


def incoming_state(message):
    slices, rows, width = message.shape
    return pl.pallas_call(
        scan_kernel,
        out_shape=jax.ShapeDtypeStruct((slices, 16, width), F32),
        in_specs=[VMEM_SPEC],
        out_specs=VMEM_SPEC,
        scratch_shapes=[
            pltpu.VMEM((slices, rows, width), F32),
            pltpu.VMEM((slices, 16, width), F32),
        ]
        + [pltpu.SemaphoreType.DMA((slices,))] * 4,
        compiler_params=pltpu.CompilerParams(collective_id=1, has_side_effects=True),
        name="scan_states",
    )(message)


def mix_kernel(d_skip, act, cum_ref, offset_ref, entry, x_ref, z_ref, gated, squares, state):
    block = pl.program_id(0)

    @pl.when(block == 0)
    def _():
        state[...] = entry[...]
        squares[...] = jnp.zeros_like(squares)

    b_in = act[:, :STATE]
    c_out = act[:, STATE:]
    x = x_ref[...]
    cum = cum_ref[...]
    offset = offset_ref[...]
    gram = dot(c_out, b_in, 1, 1)
    high, low = split(state[...])
    carried = dot(c_out, high, 1, 0) + dot(c_out, low, 1, 0)
    cum_column = jnp.transpose(cum)
    row = lax.broadcasted_iota(jnp.int32, (BLOCK, BLOCK), 0)
    column = lax.broadcasted_iota(jnp.int32, (BLOCK, BLOCK), 1)
    causal = row >= column
    for h in range(4):
        lanes = slice(h * HEAD_DIM, (h + 1) * HEAD_DIM)
        at = cum_column[:, h : h + 1]
        decay = jnp.exp(jnp.where(causal, at - offset[h : h + 1, :], -1e30))
        weights = (gram * decay).astype(BF16)
        x_head = x[:, lanes]
        out = dot(weights, x_head, 1, 0) + jnp.exp(at) * carried[:, lanes]
        out = out + d_skip[h] * x_head.astype(F32)
        out = out * jax.nn.silu(z_ref[:, lanes].astype(F32))
        gated[:, lanes] = out
    full = gated[...]
    sums = dot(jnp.ones((8, full.shape[1]), BF16), (full * full).astype(BF16), 1, 1)
    squares[pl.ds(2 * block, 1), :] = sums[0:1, 0:128]
    squares[pl.ds(2 * block + 1, 1), :] = sums[0:1, 128:256]
    state[...] = state_step(x, b_in, cum, offset, state[...])[0]


def mix(act, cum, offset, entry, x, z_gate, d_skip):
    length, width = x.shape
    by_row = lambda b: (b, 0)
    by_lane = lambda b: (0, b)
    fixed = lambda b: (0, 0)
    return pl.pallas_call(
        mix_kernel,
        grid=(length // BLOCK,),
        out_shape=(
            jax.ShapeDtypeStruct((length, width), F32),
            jax.ShapeDtypeStruct((16, 128), F32),
        ),
        in_specs=[
            SMEM_SPEC,
            pl.BlockSpec((BLOCK, 2 * STATE), by_row),
            pl.BlockSpec((8, BLOCK), by_lane),
            pl.BlockSpec((8, BLOCK), by_lane),
            pl.BlockSpec((STATE, width), fixed),
            pl.BlockSpec((BLOCK, width), by_row),
            pl.BlockSpec((BLOCK, width), by_row),
        ],
        out_specs=(pl.BlockSpec((BLOCK, width), by_row), pl.BlockSpec((16, 128), fixed)),
        scratch_shapes=[pltpu.VMEM((STATE, width), F32)],
        name="mix",
    )(d_skip, act, cum, offset, entry, x, z_gate)


def sum_kernel(part, out, pair, landed, psend, precv, zsend, zrecv):
    head = lax.axis_index("head")
    z = head // 2
    yl = head % 2
    mate = z * 2 + 1 - yl
    hops = (8, 7, 9, 6, 10, 5, 11, 4, 12, 3, 13, 2, 14, 1, 15)
    places = [(z + hop) % NZ for hop in hops]
    greet([{"head": mate}] + [{"head": place * 2 + yl} for place in places])
    first = remote(part, pair, psend, precv, head=mate)
    first.start()
    first.wait()
    landed[z] = part[...] + pair[...]
    sent = []
    for place in places:
        copy = remote(
            landed.at[z], landed.at[z], zsend.at[place], zrecv.at[z], head=place * 2 + yl
        )
        copy.start()
        sent.append(copy)
    for place in reversed(places):
        remote(
            landed.at[place],
            landed.at[place],
            zsend.at[place],
            zrecv.at[place],
            head=place * 2 + yl,
        ).wait_recv()
    total = landed[0]
    for k in range(1, NZ):
        total = total + landed[k]
    out[...] = total
    for copy in sent:
        copy.wait_send()


def sum_squares(part):
    return pl.pallas_call(
        sum_kernel,
        out_shape=jax.ShapeDtypeStruct(part.shape, F32),
        in_specs=[VMEM_SPEC],
        out_specs=VMEM_SPEC,
        scratch_shapes=[
            pltpu.VMEM(part.shape, F32),
            pltpu.VMEM((NZ,) + part.shape, F32),
            pltpu.SemaphoreType.DMA,
            pltpu.SemaphoreType.DMA,
            pltpu.SemaphoreType.DMA((NZ,)),
            pltpu.SemaphoreType.DMA((NZ,)),
        ],
        compiler_params=pltpu.CompilerParams(collective_id=2, has_side_effects=True),
        name="sum_squares",
    )(part)


def norm_kernel(squares, gain, gated, out):
    block = pl.program_id(0)
    for half in range(2):
        total = squares[pl.ds(2 * block + half, 1), :]
        inverse = lax.rsqrt(total / INNER + 1e-05)
        column = jnp.transpose(jnp.broadcast_to(inverse, (8, 128)))[:, 0:1]
        rows = slice(128 * half, 128 * half + 128)
        out[rows, :] = (gated[rows, :] * column * gain[...]).astype(BF16)


def norm(squares, gain, gated):
    length, width = gated.shape
    return pl.pallas_call(
        norm_kernel,
        grid=(length // BLOCK,),
        out_shape=jax.ShapeDtypeStruct((length, width), BF16),
        in_specs=[
            pl.BlockSpec((16, 128), lambda b: (0, 0)),
            pl.BlockSpec((1, width), lambda b: (0, 0)),
            pl.BlockSpec((BLOCK, width), lambda b: (b, 0)),
        ],
        out_specs=pl.BlockSpec((BLOCK, width), lambda b: (b, 0)),
        name="norm",
    )(squares, gain, gated)


def on_device(x_inner, z_gate, bc_raw, conv_weight, conv_bias, dt_raw, a_log, d_skip, norm_gain):
    dt = jnp.pad(dt_raw.T, ((0, 4), (0, 0)))
    gathered, rim = gather(bc_raw)
    raw = gathered.reshape(x_inner.shape[0], 2 * STATE)
    act, cum, offset, message = local_states(
        raw, rim, conv_weight, conv_bias[None, :], dt, a_log, x_inner
    )
    entry = incoming_state(message).reshape(STATE, x_inner.shape[1])
    gated, squares = mix(act, cum, offset, entry, x_inner, z_gate, d_skip)
    return norm(sum_squares(squares), norm_gain[None, :], gated)


def solution(mesh):
    placed = (
        P("seq", "head"),
        P("seq", "head"),
        P(("seq", "head"), None),
        P(),
        P(),
        P("seq", "head"),
        P("head"),
        P("head"),
        P("head"),
    )
    return jax.shard_map(
        on_device, mesh=mesh, in_specs=placed, out_specs=P("seq", "head"), check_vma=False
    )
```

```python
import jax
import jax.numpy as jnp
from jax import lax
from jax.experimental import pallas as pl
from jax.experimental.pallas import tpu as pltpu
from jax.sharding import PartitionSpec as P

HEAD_DIM = 128
STATE = 256
BLOCK = 256
INNER = 16384
NSEQ = 16
NZ = 16
VMEM_SPEC = pl.BlockSpec(memory_space=pltpu.VMEM)
SMEM_SPEC = pl.BlockSpec(memory_space=pltpu.SMEM)
F32 = jnp.float32
BF16 = jnp.bfloat16


def remote(src, dst, send, recv, **where):
    return pltpu.make_async_remote_copy(
        src_ref=src,
        dst_ref=dst,
        send_sem=send,
        recv_sem=recv,
        device_id=where,
        device_id_type=pl.DeviceIdType.MESH,
    )


def greet(targets):
    barrier = pltpu.get_barrier_semaphore()
    for where in targets:
        pl.semaphore_signal(
            barrier, inc=1, device_id=where, device_id_type=pl.DeviceIdType.MESH
        )
    pl.semaphore_wait(barrier, len(targets))


def gather_kernel(raw, out, rim, zsend, zrecv, ysend, yrecv, tsend, trecv, lsem, rsend, rrecv):
    seq = lax.axis_index("seq")
    head = lax.axis_index("head")
    z = head // 2
    yl = head % 2
    right = ((z + 1) % NZ) * 2 + yl
    left = ((z + NZ - 1) % NZ) * 2 + yl
    mate = z * 2 + 1 - yl
    after = (seq + 1) % NSEQ
    before = (seq + NSEQ - 1) % NSEQ
    greet([{"head": right}, {"head": left}, {"head": mate}, {"seq": after}, {"seq": before}])
    sides = (right, left)

    def window(turn):
        return pl.multiple_of(32 * yl + 16 * (turn + yl * (3 - 2 * turn)), 16)

    def span(start, size):
        return pl.ds(pl.multiple_of(start, 16), size)

    def ring(side, step, turn, slot, src):
        return remote(
            src,
            out.at[slot, span(window(turn), 16)],
            zsend.at[side, step, turn],
            zrecv.at[side, step, turn],
            head=sides[side],
        )

    def across(index, slot, src):
        return remote(
            src,
            out.at[slot, span(64 * yl, 32)],
            ysend.at[index],
            yrecv.at[index],
            head=mate,
        )

    sent = []

    def go(copy):
        copy.start()
        sent.append(copy)

    middle = remote(
        raw.at[span(32 - 32 * yl, 16)],
        out.at[z, span(32 + 16 * yl, 16)],
        tsend,
        trecv,
        head=mate,
    )
    go(middle)
    for turn in range(3):
        for side in range(2):
            go(ring(side, 0, turn, z, raw.at[span(window(turn) - 48 * yl, 16)]))
    go(across(0, z, raw.at[span(16 * yl, 32)]))
    own = pltpu.make_async_copy(raw, out.at[z, span(48 * yl, 48)], lsem)
    own.start()
    remote(
        raw.at[span(32 - 32 * yl, 16)],
        out.at[z, span(48 - 16 * yl, 16)],
        tsend,
        trecv,
        head=mate,
    ).wait_recv()
    for side in range(2):
        go(ring(side, 0, 3, z, out.at[z, span(window(3), 16)]))
    for step in range(1, 9):
        slots = ((z + NZ - step) % NZ, (z + step) % NZ)
        for turn in range(4):
            for side in range(2):
                if step == 8 and side != turn // 2:
                    continue
                slot = slots[side]
                piece = out.at[slot, span(window(turn), 16)]
                ring(side, step - 1, turn, slot, piece).wait_recv()
                if step < 7 or (step == 7 and side == turn // 2):
                    go(ring(side, step, turn, slot, piece))
                if turn == 1:
                    index = step + 8 * side
                    go(across(index, slot, out.at[slot, span(64 * yl, 32)]))
    for index in range(16):
        slot = (z + NZ - index) % NZ if index <= 8 else (z + index - 8) % NZ
        landed = out.at[slot, span(64 * (1 - yl), 32)]
        remote(landed, landed, ysend.at[index], yrecv.at[index], head=mate).wait_recv()
    own.wait()
    edge = remote(out.at[NZ - 1, pl.ds(80, 16)], rim, rsend, rrecv, seq=after)
    edge.start()
    for copy in sent:
        copy.wait_send()
    edge.wait()


def gather(raw):
    rows, width = raw.shape
    return pl.pallas_call(
        gather_kernel,
        out_shape=(
            jax.ShapeDtypeStruct((NZ, 2 * rows, width), raw.dtype),
            jax.ShapeDtypeStruct((16, width), raw.dtype),
        ),
        in_specs=[VMEM_SPEC],
        out_specs=(VMEM_SPEC, VMEM_SPEC),
        scratch_shapes=[
            pltpu.SemaphoreType.DMA((2, 8, 4)),
            pltpu.SemaphoreType.DMA((2, 8, 4)),
            pltpu.SemaphoreType.DMA((16,)),
            pltpu.SemaphoreType.DMA((16,)),
            pltpu.SemaphoreType.DMA,
            pltpu.SemaphoreType.DMA,
            pltpu.SemaphoreType.DMA,
            pltpu.SemaphoreType.DMA,
            pltpu.SemaphoreType.DMA,
        ],
        compiler_params=pltpu.CompilerParams(collective_id=0, has_side_effects=True),
        name="gather_bc",
    )(raw)


def split(value):
    high = value.astype(BF16)
    return high, (value - high.astype(F32)).astype(BF16)


def dot(a, b, ca, cb):
    return lax.dot_general(a, b, (((ca,), (cb,)), ((), ())), preferred_element_type=F32)


def spread_heads(column):
    rows = column.shape[0]
    return jnp.concatenate(
        [jnp.broadcast_to(column[:, h : h + 1], (rows, HEAD_DIM)) for h in range(4)], axis=1
    )


def lane_row(tile):
    return jnp.concatenate([tile[h : h + 1, :] for h in range(4)], axis=1)


def mixer_kernel(
    a_log,
    d_skip,
    raw,
    rim,
    conv_weight,
    conv_bias,
    dt,
    gain,
    x_far,
    z_far,
    out,
    x_ref,
    z_ref,
    act,
    padded,
    cums,
    offsets,
    starts,
    priors,
    state,
    total,
    mixed,
    message,
    fade,
    landed,
    fades,
    prefix,
    entry,
    squares,
    pair,
    parts,
    local_sem,
    fsend,
    frecv,
    asend,
    arecv,
    bsend,
    brecv,
    psend,
    precv,
    zsend,
    zrecv,
):
    seq = lax.axis_index("seq")
    head = lax.axis_index("head")
    z = head // 2
    yl = head % 2
    mate = z * 2 + 1 - yl
    blocks = x_ref.shape[0] // BLOCK
    others = [(seq + hop) % NSEQ for hop in (10, 6, 14, 11, 9, 5, 13, 7, 15, 3, 8, 12, 4, 2, 1)]
    hops = (8, 7, 9, 6, 10, 5, 11, 4, 12, 3, 13, 2, 14, 1, 15)
    places = [(z + hop) % NZ for hop in hops]
    targets = [{"seq": other} for other in others] + [{"head": mate}]
    targets = targets + [{"head": place * 2 + yl} for place in places]
    barrier = pltpu.get_barrier_semaphore()
    for where in targets:
        pl.semaphore_signal(
            barrier, inc=1, device_id=where, device_id_type=pl.DeviceIdType.MESH
        )
    fetch_x = pltpu.make_async_copy(x_far, x_ref, local_sem.at[0])
    fetch_z = pltpu.make_async_copy(z_far, z_ref, local_sem.at[1])
    fetch_x.start()
    fetch_z.start()

    def rows_of(block):
        return pl.ds(pl.multiple_of(block * BLOCK, BLOCK), BLOCK)

    sub = lax.broadcasted_iota(jnp.int32, (8, BLOCK), 0)
    rate = jnp.full((8, BLOCK), a_log[0], F32)
    for h in range(1, 4):
        rate = jnp.where(sub == h, a_log[h], rate)
    rate = -jnp.exp(rate)
    row = lax.broadcasted_iota(jnp.int32, (BLOCK, BLOCK), 0)
    column = lax.broadcasted_iota(jnp.int32, (BLOCK, BLOCK), 1)
    upper = jnp.where(row <= column, 1.0, 0.0).astype(BF16)
    padded[0:8, :] = jnp.where(seq == 0, 0.0, rim[...].astype(F32)[8:16, :])
    state[...] = jnp.zeros_like(state)
    total[...] = jnp.zeros_like(total)
    squares[...] = jnp.zeros_like(squares)
    fetch_x.wait()

    def first_pass(block, _):
        rows = rows_of(block)
        padded[8 : 8 + BLOCK, :] = raw[rows, :].astype(F32)
        summed = jnp.broadcast_to(conv_bias[...], (BLOCK, 2 * STATE))
        for tap in range(4):
            summed = summed + conv_weight[tap : tap + 1, :] * padded[5 + tap : 5 + tap + BLOCK, :]
        acted = jax.nn.silu(summed).astype(BF16)
        act[rows, :] = acted
        padded[0:8, :] = padded[BLOCK : BLOCK + 8, :]
        raw_dt = dt[block]
        size = jnp.maximum(raw_dt, 0.0) + jnp.log1p(jnp.exp(-jnp.abs(raw_dt)))
        log_step = rate * size
        high = log_step.astype(BF16)
        middle, low = split(log_step - high.astype(F32))
        cum = (dot(low, upper, 1, 0) + dot(middle, upper, 1, 0)) + dot(high, upper, 1, 0)
        offset = cum - jnp.log(size)
        cums[block] = cum
        offsets[block] = offset
        last = cum[:, BLOCK - 1 : BLOCK]
        tail = jnp.exp(jnp.transpose(last - offset))
        high, low = split(x_ref[rows, :].astype(F32) * spread_heads(tail))
        b_in = acted[:, :STATE]
        ends = jnp.broadcast_to(last, (8, 128))
        starts[block] = state[...]
        priors[block] = jnp.exp(total[...])
        fresh = dot(b_in, high, 0, 0) + dot(b_in, low, 0, 0)
        state[...] = lane_row(jnp.exp(ends)) * state[...] + fresh
        total[...] = total[...] + ends
        return 0

    lax.fori_loop(0, blocks, first_pass, 0)
    for k in range(NSEQ):
        message[k] = state[16 * k : 16 * k + 16, :].astype(BF16)
    fade[...] = jnp.exp(total[...])
    pl.semaphore_wait(barrier, len(targets))
    sent = []
    for other in others:
        copy = remote(fade, fades.at[seq], fsend.at[other], frecv.at[seq], seq=other)
        copy.start()
        sent.append(copy)
        copy = remote(message.at[other], landed.at[seq], asend.at[other], arecv.at[seq], seq=other)
        copy.start()
        sent.append(copy)
    landed[seq] = message[seq]
    fades[seq] = fade[...]

    causal = row >= column

    def inner_pass(block, _):
        rows = rows_of(block)
        gram = dot(act[rows, STATE:], act[rows, :STATE], 1, 1)
        at_all = jnp.transpose(cums[block])
        offset = offsets[block]
        for h in range(4):
            lanes = slice(h * HEAD_DIM, (h + 1) * HEAD_DIM)
            gap = at_all[:, h : h + 1] - offset[h : h + 1, :]
            decay = jnp.exp(jnp.where(causal, gap, -1e30))
            x_head = x_ref[rows, lanes]
            mixed[rows, lanes] = dot(
                (gram * decay).astype(BF16), x_head, 1, 0
            ) + d_skip[h] * x_head.astype(F32)
        return 0

    lax.fori_loop(0, blocks // 2, inner_pass, 0)
    for other in others:
        remote(fades.at[other], fades.at[other], fsend.at[other], frecv.at[other], seq=other).wait_recv()
        remote(
            landed.at[other], landed.at[other], asend.at[other], arecv.at[other], seq=other
        ).wait_recv()
    running = jnp.zeros((16, x_ref.shape[1]), F32)
    for s in range(NSEQ):
        prefix[s] = running.astype(BF16)
        if s < NSEQ - 1:
            running = lane_row(fades[s]) * running + landed[s].astype(F32)
    for other in others:
        copy = remote(prefix.at[other], entry.at[seq], bsend.at[other], brecv.at[seq], seq=other)
        copy.start()
        sent.append(copy)
    entry[seq] = prefix[seq]
    lax.fori_loop(blocks // 2, blocks, inner_pass, 0)
    fetch_z.wait()
    for other in others:
        remote(
            entry.at[other], entry.at[other], bsend.at[other], brecv.at[other], seq=other
        ).wait_recv()
    state[...] = entry[...].astype(F32).reshape(state.shape)
    ones = jnp.ones((8, x_ref.shape[1]), BF16)

    def last_pass(block, _):
        rows = rows_of(block)
        high, low = split(starts[block] + lane_row(priors[block]) * state[...])
        c_out = act[rows, STATE:]
        carried = dot(c_out, high, 1, 0) + dot(c_out, low, 1, 0)
        scale = spread_heads(jnp.exp(jnp.transpose(cums[block])))
        gate = jax.nn.silu(z_ref[rows, :].astype(F32))
        gated = (mixed[rows, :] + scale * carried) * gate
        mixed[rows, :] = gated
        sums = dot(ones, (gated * gated).astype(BF16), 1, 1)
        squares[pl.ds(2 * block, 1), :] = sums[0:1, 0:128]
        squares[pl.ds(2 * block + 1, 1), :] = sums[0:1, 128:256]
        return 0

    lax.fori_loop(0, blocks, last_pass, 0)
    first = remote(squares, pair, psend, precv, head=mate)
    first.start()
    first.wait()
    parts[z] = squares[...] + pair[...]
    for place in places:
        copy = remote(
            parts.at[z], parts.at[z], zsend.at[place], zrecv.at[z], head=place * 2 + yl
        )
        copy.start()
        sent.append(copy)
    for place in reversed(places):
        remote(
            parts.at[place], parts.at[place], zsend.at[place], zrecv.at[place], head=place * 2 + yl
        ).wait_recv()
    whole = parts[0]
    for k in range(1, NZ):
        whole = whole + parts[k]
    pair[...] = lax.rsqrt(whole / INNER + 1e-05)

    def norm_pass(part, _):
        rows = pl.ds(pl.multiple_of(part * 128, 128), 128)
        inverse = jnp.transpose(jnp.broadcast_to(pair[pl.ds(part, 1), :], (8, 128)))[:, 0:1]
        out[rows, :] = (mixed[rows, :] * inverse * gain[...]).astype(BF16)
        return 0

    lax.fori_loop(0, 2 * blocks, norm_pass, 0)
    for copy in sent:
        copy.wait_send()


def mixer(raw, rim, conv_weight, conv_bias, dt, a_log, d_skip, gain, x, z_gate):
    length, width = x.shape
    blocks = length // BLOCK
    far = pl.BlockSpec(memory_space=pl.ANY)
    dma = pltpu.SemaphoreType.DMA
    return pl.pallas_call(
        mixer_kernel,
        out_shape=jax.ShapeDtypeStruct((length, width), BF16),
        in_specs=[SMEM_SPEC, SMEM_SPEC] + [VMEM_SPEC] * 6 + [far, far],
        out_specs=VMEM_SPEC,
        scratch_shapes=[
            pltpu.VMEM((length, width), BF16),
            pltpu.VMEM((length, width), BF16),
            pltpu.VMEM((length, 2 * STATE), BF16),
            pltpu.VMEM((BLOCK + 8, 2 * STATE), F32),
            pltpu.VMEM((blocks, 8, BLOCK), F32),
            pltpu.VMEM((blocks, 8, BLOCK), F32),
            pltpu.VMEM((blocks, STATE, width), F32),
            pltpu.VMEM((blocks, 8, 128), F32),
            pltpu.VMEM((STATE, width), F32),
            pltpu.VMEM((8, 128), F32),
            pltpu.VMEM((length, width), F32),
            pltpu.VMEM((NSEQ, 16, width), BF16),
            pltpu.VMEM((8, 128), F32),
            pltpu.VMEM((NSEQ, 16, width), BF16),
            pltpu.VMEM((NSEQ, 8, 128), F32),
            pltpu.VMEM((NSEQ, 16, width), BF16),
            pltpu.VMEM((NSEQ, 16, width), BF16),
            pltpu.VMEM((16, 128), F32),
            pltpu.VMEM((16, 128), F32),
            pltpu.VMEM((NZ, 16, 128), F32),
            dma((2,)),
        ]
        + [dma((NSEQ,))] * 6
        + [dma, dma, dma((NZ,)), dma((NZ,))],
        compiler_params=pltpu.CompilerParams(
            collective_id=1, has_side_effects=True, vmem_limit_bytes=48 * 1024 * 1024
        ),
        name="mixer",
    )(a_log, d_skip, raw, rim, conv_weight, conv_bias, dt, gain, x, z_gate)


def on_device(x_inner, z_gate, bc_raw, conv_weight, conv_bias, dt_raw, a_log, d_skip, norm_gain):
    length = x_inner.shape[0]
    dt = jnp.pad(dt_raw.T, ((0, 4), (0, 0)))
    dt = jnp.transpose(dt.reshape(8, length // BLOCK, BLOCK), (1, 0, 2))
    gathered, rim = gather(bc_raw)
    raw = gathered.reshape(length, 2 * STATE)
    return mixer(
        raw,
        rim,
        conv_weight,
        conv_bias[None, :],
        dt,
        a_log,
        d_skip,
        norm_gain[None, :],
        x_inner,
        z_gate,
    )


def solution(mesh):
    placed = (
        P("seq", "head"),
        P("seq", "head"),
        P(("seq", "head"), None),
        P(),
        P(),
        P("seq", "head"),
        P("head"),
        P("head"),
        P("head"),
    )
    return jax.shard_map(
        on_device, mesh=mesh, in_specs=placed, out_specs=P("seq", "head"), check_vma=False
    )
```

```python
import jax
import jax.numpy as jnp
from jax import lax
from jax.experimental import pallas as pl
from jax.experimental.pallas import tpu as pltpu
from jax.sharding import PartitionSpec as P

HEAD_DIM = 128
STATE = 256
BLOCK = 256
INNER = 16384
NSEQ = 16
NZ = 16
VMEM_SPEC = pl.BlockSpec(memory_space=pltpu.VMEM)
SMEM_SPEC = pl.BlockSpec(memory_space=pltpu.SMEM)
F32 = jnp.float32
BF16 = jnp.bfloat16


def remote(src, dst, send, recv, **where):
    return pltpu.make_async_remote_copy(
        src_ref=src,
        dst_ref=dst,
        send_sem=send,
        recv_sem=recv,
        device_id=where,
        device_id_type=pl.DeviceIdType.MESH,
    )


def greet(targets):
    barrier = pltpu.get_barrier_semaphore()
    for where in targets:
        pl.semaphore_signal(
            barrier, inc=1, device_id=where, device_id_type=pl.DeviceIdType.MESH
        )
    pl.semaphore_wait(barrier, len(targets))


def gather_kernel(raw, out, rim, zsend, zrecv, ysend, yrecv, lsem, rootsend, rsend, rrecv):
    seq = lax.axis_index("seq")
    head = lax.axis_index("head")
    z = head // 2
    yl = head % 2
    mate = z * 2 + 1 - yl
    after = (seq + 1) % NSEQ
    before = (seq + NSEQ - 1) % NSEQ
    is_root = head == 2 * NZ - 1
    is_relay = (yl == 1) & (z % 4 == 3)
    relay = ((4 * ((z + 2) // 4) + NZ - 1) % NZ) * 2 + 1

    def along(side, by):
        return ((z + (by if side == 0 else NZ - by)) % NZ) * 2 + yl

    barrier = pltpu.get_barrier_semaphore()

    def greet_one(where):
        pl.semaphore_signal(
            barrier, inc=1, device_id=where, device_id_type=pl.DeviceIdType.MESH
        )

    for side in range(2):
        for by in (1, 2):
            greet_one({"head": along(side, by)})
    greet_one({"head": mate})

    @pl.when(is_relay)
    def _():
        greet_one({"seq": before, "head": 2 * NZ - 1})

    @pl.when(jnp.logical_not(is_relay))
    def _():
        greet_one({"head": relay})

    pl.semaphore_wait(
        barrier, 5 + 4 * is_root.astype(jnp.int32) + 7 * is_relay.astype(jnp.int32)
    )

    own_rows = pl.ds(pl.multiple_of(48 * yl, 16), 48)
    mate_rows = pl.ds(pl.multiple_of(48 - 48 * yl, 16), 48)

    def slot_of(side, far):
        return (z + (NZ - far if side == 0 else far)) % NZ

    def hop(side, far, slot, first=False):
        start, size = (48 * yl, 48) if far < 8 else (48 * yl + 32 * side, 32 - 16 * side)
        rows = pl.ds(pl.multiple_of(start, 16), size)
        there = out.at[slot, rows]
        return remote(
            raw if first else there,
            there,
            zsend.at[side, far],
            zrecv.at[side, far],
            head=along(side, 1 if far == 1 else 2),
        )

    def across(index, slot, src=None):
        there = out.at[slot, own_rows]
        return remote(
            there if src is None else src, there, ysend.at[index], yrecv.at[index], head=mate
        )

    sent = []

    def go(copy):
        copy.start()
        sent.append(copy)

    for side in range(2):
        go(hop(side, 2, z, True))
        go(hop(side, 1, z, True))
    go(across(0, z, raw))

    def from_root(group):
        return remote(
            raw.at[pl.ds(32, 16)],
            rim,
            rootsend.at[group],
            rrecv,
            seq=after,
            head=(4 * group + 3) * 2 + 1,
        )

    def from_relay(index):
        by, column = ((0, 0), (1, 0), (1, 1), (2, 0), (2, 1), (NZ - 1, 0), (NZ - 1, 1))[index]
        return remote(rim, rim, rsend.at[index], rrecv, head=((z + by) % NZ) * 2 + column)

    @pl.when(is_root)
    def _():
        for group in range(4):
            from_root(group).start()

    own = pltpu.make_async_copy(raw, out.at[z, own_rows], lsem)
    own.start()
    for far in range(1, 9):
        for side in range(2):
            slot = slot_of(side, far)
            hop(side, far, slot).wait_recv()
            if far + 2 <= 8:
                go(hop(side, far + 2, slot))
            if far < 8:
                go(across(far + 8 * side, slot))
        if far == 6:

            @pl.when(is_relay)
            def _():
                from_root(0).wait_recv()
                for index in range(7):
                    from_relay(index).start()

    go(across(8, slot_of(0, 8)))
    for index in range(16):
        slot = slot_of(0, index) if index <= 8 else slot_of(1, index - 8)
        landed = out.at[slot, mate_rows]
        remote(landed, landed, ysend.at[index], yrecv.at[index], head=mate).wait_recv()
    own.wait()

    @pl.when(jnp.logical_not(is_relay))
    def _():
        from_root(0).wait_recv()

    @pl.when(is_relay)
    def _():
        for index in range(7):
            from_relay(index).wait_send()

    @pl.when(is_root)
    def _():
        for group in range(4):
            from_root(group).wait_send()

    for copy in sent:
        copy.wait_send()


def gather(raw):
    rows, width = raw.shape
    dma = pltpu.SemaphoreType.DMA
    return pl.pallas_call(
        gather_kernel,
        out_shape=(
            jax.ShapeDtypeStruct((NZ, 2 * rows, width), raw.dtype),
            jax.ShapeDtypeStruct((16, width), raw.dtype),
        ),
        in_specs=[VMEM_SPEC],
        out_specs=(VMEM_SPEC, VMEM_SPEC),
        scratch_shapes=[
            dma((2, 9)),
            dma((2, 9)),
            dma((16,)),
            dma((16,)),
            dma,
            dma((4,)),
            dma((7,)),
            dma,
        ],
        compiler_params=pltpu.CompilerParams(
            collective_id=0, has_side_effects=True, vmem_limit_bytes=8 * 1024 * 1024
        ),
        name="gather_bc",
    )(raw)


def split(value):
    high = value.astype(BF16)
    return high, (value - high.astype(F32)).astype(BF16)


def dot(a, b, ca, cb):
    return lax.dot_general(a, b, (((ca,), (cb,)), ((), ())), preferred_element_type=F32)


def spread_heads(column):
    rows = column.shape[0]
    return jnp.concatenate(
        [jnp.broadcast_to(column[:, h : h + 1], (rows, HEAD_DIM)) for h in range(4)], axis=1
    )


def lane_row(tile):
    return jnp.concatenate([tile[h : h + 1, :] for h in range(4)], axis=1)


def mixer_kernel(
    a_log,
    d_skip,
    raw,
    rim,
    conv_weight,
    conv_bias,
    dt,
    gain,
    x_far,
    z_far,
    out,
    x_ref,
    z_ref,
    act,
    padded,
    cums,
    offsets,
    starts,
    priors,
    state,
    total,
    mixed,
    message,
    fade,
    landed,
    fades,
    prefix,
    entry,
    squares,
    pair,
    parts,
    local_sem,
    fsend,
    frecv,
    asend,
    arecv,
    bsend,
    brecv,
    psend,
    precv,
    zsend,
    zrecv,
):
    seq = lax.axis_index("seq")
    head = lax.axis_index("head")
    z = head // 2
    yl = head % 2
    mate = z * 2 + 1 - yl
    blocks = x_ref.shape[0] // BLOCK
    others = [(seq + hop) % NSEQ for hop in (10, 6, 14, 11, 9, 5, 13, 7, 15, 3, 8, 12, 4, 2, 1)]
    hops = (8, 7, 9, 6, 10, 5, 11, 4, 12, 3, 13, 2, 14, 1, 15)
    places = [(z + hop) % NZ for hop in hops]
    targets = [{"seq": other} for other in others] + [{"head": mate}]
    targets = targets + [{"head": place * 2 + yl} for place in places]
    barrier = pltpu.get_barrier_semaphore()
    for where in targets:
        pl.semaphore_signal(
            barrier, inc=1, device_id=where, device_id_type=pl.DeviceIdType.MESH
        )
    fetch_x = pltpu.make_async_copy(x_far, x_ref, local_sem.at[0])
    fetch_z = pltpu.make_async_copy(z_far, z_ref, local_sem.at[1])
    fetch_x.start()
    fetch_z.start()

    def rows_of(block):
        return pl.ds(pl.multiple_of(block * BLOCK, BLOCK), BLOCK)

    sub = lax.broadcasted_iota(jnp.int32, (8, BLOCK), 0)
    rate = jnp.full((8, BLOCK), a_log[0], F32)
    for h in range(1, 4):
        rate = jnp.where(sub == h, a_log[h], rate)
    rate = -jnp.exp(rate)
    row = lax.broadcasted_iota(jnp.int32, (BLOCK, BLOCK), 0)
    column = lax.broadcasted_iota(jnp.int32, (BLOCK, BLOCK), 1)
    upper = jnp.where(row <= column, 1.0, 0.0).astype(BF16)
    padded[0:8, :] = jnp.where(seq == 0, 0.0, rim[...].astype(F32)[8:16, :])
    state[...] = jnp.zeros_like(state)
    total[...] = jnp.zeros_like(total)
    squares[...] = jnp.zeros_like(squares)
    fetch_x.wait()

    def first_pass(block, _):
        rows = rows_of(block)
        padded[8 : 8 + BLOCK, :] = raw[rows, :].astype(F32)
        summed = jnp.broadcast_to(conv_bias[...], (BLOCK, 2 * STATE))
        for tap in range(4):
            summed = summed + conv_weight[tap : tap + 1, :] * padded[5 + tap : 5 + tap + BLOCK, :]
        acted = jax.nn.silu(summed).astype(BF16)
        act[rows, :] = acted
        padded[0:8, :] = padded[BLOCK : BLOCK + 8, :]
        raw_dt = dt[block]
        size = jnp.maximum(raw_dt, 0.0) + jnp.log1p(jnp.exp(-jnp.abs(raw_dt)))
        log_step = rate * size
        high = log_step.astype(BF16)
        middle, low = split(log_step - high.astype(F32))
        cum = (dot(low, upper, 1, 0) + dot(middle, upper, 1, 0)) + dot(high, upper, 1, 0)
        offset = cum - jnp.log(size)
        cums[block] = cum
        offsets[block] = offset
        last = cum[:, BLOCK - 1 : BLOCK]
        tail = jnp.exp(jnp.transpose(last - offset))
        high, low = split(x_ref[rows, :].astype(F32) * spread_heads(tail))
        b_in = acted[:, :STATE]
        ends = jnp.broadcast_to(last, (8, 128))
        starts[block] = state[...]
        priors[block] = jnp.exp(total[...])
        fresh = dot(b_in, high, 0, 0) + dot(b_in, low, 0, 0)
        state[...] = lane_row(jnp.exp(ends)) * state[...] + fresh
        total[...] = total[...] + ends
        return 0

    lax.fori_loop(0, blocks, first_pass, 0)
    for k in range(NSEQ):
        message[k] = state[16 * k : 16 * k + 16, :].astype(BF16)
    fade[...] = jnp.exp(total[...])
    pl.semaphore_wait(barrier, len(targets))
    sent = []
    for other in others:
        copy = remote(fade, fades.at[seq], fsend.at[other], frecv.at[seq], seq=other)
        copy.start()
        sent.append(copy)
        copy = remote(message.at[other], landed.at[seq], asend.at[other], arecv.at[seq], seq=other)
        copy.start()
        sent.append(copy)
    landed[seq] = message[seq]
    fades[seq] = fade[...]

    causal = row >= column

    def inner_pass(block, _):
        rows = rows_of(block)
        gram = dot(act[rows, STATE:], act[rows, :STATE], 1, 1)
        at_all = jnp.transpose(cums[block])
        offset = offsets[block]
        for h in range(4):
            lanes = slice(h * HEAD_DIM, (h + 1) * HEAD_DIM)
            gap = at_all[:, h : h + 1] - offset[h : h + 1, :]
            decay = jnp.exp(jnp.where(causal, gap, -1e30))
            x_head = x_ref[rows, lanes]
            mixed[rows, lanes] = dot(
                (gram * decay).astype(BF16), x_head, 1, 0
            ) + d_skip[h] * x_head.astype(F32)
        return 0

    lax.fori_loop(0, blocks // 2, inner_pass, 0)
    for other in others:
        remote(fades.at[other], fades.at[other], fsend.at[other], frecv.at[other], seq=other).wait_recv()
        remote(
            landed.at[other], landed.at[other], asend.at[other], arecv.at[other], seq=other
        ).wait_recv()
    running = jnp.zeros((16, x_ref.shape[1]), F32)
    for s in range(NSEQ):
        prefix[s] = running.astype(BF16)
        if s < NSEQ - 1:
            running = lane_row(fades[s]) * running + landed[s].astype(F32)
    for other in others:
        copy = remote(prefix.at[other], entry.at[seq], bsend.at[other], brecv.at[seq], seq=other)
        copy.start()
        sent.append(copy)
    entry[seq] = prefix[seq]
    lax.fori_loop(blocks // 2, blocks, inner_pass, 0)
    fetch_z.wait()
    for other in others:
        remote(
            entry.at[other], entry.at[other], bsend.at[other], brecv.at[other], seq=other
        ).wait_recv()
    state[...] = entry[...].astype(F32).reshape(state.shape)
    ones = jnp.ones((8, x_ref.shape[1]), BF16)

    def last_pass(block, _):
        rows = rows_of(block)
        high, low = split(starts[block] + lane_row(priors[block]) * state[...])
        c_out = act[rows, STATE:]
        carried = dot(c_out, high, 1, 0) + dot(c_out, low, 1, 0)
        scale = spread_heads(jnp.exp(jnp.transpose(cums[block])))
        gate = jax.nn.silu(z_ref[rows, :].astype(F32))
        gated = (mixed[rows, :] + scale * carried) * gate
        mixed[rows, :] = gated
        sums = dot(ones, (gated * gated).astype(BF16), 1, 1)
        squares[pl.ds(2 * block, 1), :] = sums[0:1, 0:128]
        squares[pl.ds(2 * block + 1, 1), :] = sums[0:1, 128:256]
        return 0

    lax.fori_loop(0, blocks, last_pass, 0)
    first = remote(squares, pair, psend, precv, head=mate)
    first.start()
    first.wait()
    parts[z] = squares[...] + pair[...]
    for place in places:
        copy = remote(
            parts.at[z], parts.at[z], zsend.at[place], zrecv.at[z], head=place * 2 + yl
        )
        copy.start()
        sent.append(copy)
    for place in reversed(places):
        remote(
            parts.at[place], parts.at[place], zsend.at[place], zrecv.at[place], head=place * 2 + yl
        ).wait_recv()
    whole = parts[0]
    for k in range(1, NZ):
        whole = whole + parts[k]
    pair[...] = lax.rsqrt(whole / INNER + 1e-05)

    def norm_pass(part, _):
        rows = pl.ds(pl.multiple_of(part * 128, 128), 128)
        inverse = jnp.transpose(jnp.broadcast_to(pair[pl.ds(part, 1), :], (8, 128)))[:, 0:1]
        out[rows, :] = (mixed[rows, :] * inverse * gain[...]).astype(BF16)
        return 0

    lax.fori_loop(0, 2 * blocks, norm_pass, 0)
    for copy in sent:
        copy.wait_send()


def mixer(raw, rim, conv_weight, conv_bias, dt, a_log, d_skip, gain, x, z_gate):
    length, width = x.shape
    blocks = length // BLOCK
    far = pl.BlockSpec(memory_space=pl.ANY)
    dma = pltpu.SemaphoreType.DMA
    return pl.pallas_call(
        mixer_kernel,
        out_shape=jax.ShapeDtypeStruct((length, width), BF16),
        in_specs=[SMEM_SPEC, SMEM_SPEC] + [VMEM_SPEC] * 6 + [far, far],
        out_specs=VMEM_SPEC,
        scratch_shapes=[
            pltpu.VMEM((length, width), BF16),
            pltpu.VMEM((length, width), BF16),
            pltpu.VMEM((length, 2 * STATE), BF16),
            pltpu.VMEM((BLOCK + 8, 2 * STATE), F32),
            pltpu.VMEM((blocks, 8, BLOCK), F32),
            pltpu.VMEM((blocks, 8, BLOCK), F32),
            pltpu.VMEM((blocks, STATE, width), F32),
            pltpu.VMEM((blocks, 8, 128), F32),
            pltpu.VMEM((STATE, width), F32),
            pltpu.VMEM((8, 128), F32),
            pltpu.VMEM((length, width), F32),
            pltpu.VMEM((NSEQ, 16, width), BF16),
            pltpu.VMEM((8, 128), F32),
            pltpu.VMEM((NSEQ, 16, width), BF16),
            pltpu.VMEM((NSEQ, 8, 128), F32),
            pltpu.VMEM((NSEQ, 16, width), BF16),
            pltpu.VMEM((NSEQ, 16, width), BF16),
            pltpu.VMEM((16, 128), F32),
            pltpu.VMEM((16, 128), F32),
            pltpu.VMEM((NZ, 16, 128), F32),
            dma((2,)),
        ]
        + [dma((NSEQ,))] * 6
        + [dma, dma, dma((NZ,)), dma((NZ,))],
        compiler_params=pltpu.CompilerParams(
            collective_id=1, has_side_effects=True, vmem_limit_bytes=48 * 1024 * 1024
        ),
        name="mixer",
    )(a_log, d_skip, raw, rim, conv_weight, conv_bias, dt, gain, x, z_gate)


def on_device(x_inner, z_gate, bc_raw, conv_weight, conv_bias, dt_raw, a_log, d_skip, norm_gain):
    length = x_inner.shape[0]
    dt = jnp.pad(dt_raw.T, ((0, 4), (0, 0)))
    dt = jnp.transpose(dt.reshape(8, length // BLOCK, BLOCK), (1, 0, 2))
    gathered, rim = gather(bc_raw)
    raw = gathered.reshape(length, 2 * STATE)
    return mixer(
        raw,
        rim,
        conv_weight,
        conv_bias[None, :],
        dt,
        a_log,
        d_skip,
        norm_gain[None, :],
        x_inner,
        z_gate,
    )


def solution(mesh):
    placed = (
        P("seq", "head"),
        P("seq", "head"),
        P(("seq", "head"), None),
        P(),
        P(),
        P("seq", "head"),
        P("head"),
        P("head"),
        P("head"),
    )
    return jax.shard_map(
        on_device, mesh=mesh, in_specs=placed, out_specs=P("seq", "head"), check_vma=False
    )
```

```python
import jax
import jax.numpy as jnp
from jax import lax
from jax.experimental import pallas as pl
from jax.experimental.pallas import tpu as pltpu
from jax.sharding import PartitionSpec as P

HEAD_DIM = 128
STATE = 256
BLOCK = 256
INNER = 16384
NSEQ = 16
NZ = 16
VMEM_SPEC = pl.BlockSpec(memory_space=pltpu.VMEM)
F32 = jnp.float32
BF16 = jnp.bfloat16


def remote(src, dst, send, recv, **where):
    return pltpu.make_async_remote_copy(
        src_ref=src,
        dst_ref=dst,
        send_sem=send,
        recv_sem=recv,
        device_id=where,
        device_id_type=pl.DeviceIdType.MESH,
    )


def greet(targets):
    barrier = pltpu.get_barrier_semaphore()
    for where in targets:
        pl.semaphore_signal(
            barrier, inc=1, device_id=where, device_id_type=pl.DeviceIdType.MESH
        )
    pl.semaphore_wait(barrier, len(targets))


def gather_kernel(raw, out, rim, zsend, zrecv, ysend, yrecv, lsem, rootsend, rsend, rrecv):
    seq = lax.axis_index("seq")
    head = lax.axis_index("head")
    z = head // 2
    yl = head % 2
    mate = z * 2 + 1 - yl
    after = (seq + 1) % NSEQ
    before = (seq + NSEQ - 1) % NSEQ
    is_root = head == 2 * NZ - 1
    is_relay = (yl == 1) & (z % 4 == 3)
    relay = ((4 * ((z + 2) // 4) + NZ - 1) % NZ) * 2 + 1

    def along(side, by):
        return ((z + (by if side == 0 else NZ - by)) % NZ) * 2 + yl

    barrier = pltpu.get_barrier_semaphore()

    def greet_one(where):
        pl.semaphore_signal(
            barrier, inc=1, device_id=where, device_id_type=pl.DeviceIdType.MESH
        )

    for side in range(2):
        for by in (1, 2):
            greet_one({"head": along(side, by)})
    greet_one({"head": mate})

    @pl.when(is_relay)
    def _():
        greet_one({"seq": before, "head": 2 * NZ - 1})

    @pl.when(jnp.logical_not(is_relay))
    def _():
        greet_one({"head": relay})

    pl.semaphore_wait(
        barrier, 5 + 4 * is_root.astype(jnp.int32) + 7 * is_relay.astype(jnp.int32)
    )

    own_rows = pl.ds(pl.multiple_of(48 * yl, 16), 48)
    mate_rows = pl.ds(pl.multiple_of(48 - 48 * yl, 16), 48)

    def slot_of(side, far):
        return (z + (NZ - far if side == 0 else far)) % NZ

    def hop(side, far, slot, first=False):
        start, size = (48 * yl, 48) if far < 8 else (48 * yl + 32 * side, 32 - 16 * side)
        rows = pl.ds(pl.multiple_of(start, 16), size)
        there = out.at[slot, rows]
        return remote(
            raw if first else there,
            there,
            zsend.at[side, far],
            zrecv.at[side, far],
            head=along(side, 1 if far == 1 else 2),
        )

    def across(index, slot, src=None):
        there = out.at[slot, own_rows]
        return remote(
            there if src is None else src, there, ysend.at[index], yrecv.at[index], head=mate
        )

    sent = []

    def go(copy):
        copy.start()
        sent.append(copy)

    for side in range(2):
        go(hop(side, 2, z, True))
        go(hop(side, 1, z, True))
    go(across(0, z, raw))

    def from_root(group):
        return remote(
            raw.at[pl.ds(32, 16)],
            rim,
            rootsend.at[group],
            rrecv,
            seq=after,
            head=(4 * group + 3) * 2 + 1,
        )

    def from_relay(index):
        by, column = ((0, 0), (1, 0), (1, 1), (2, 0), (2, 1), (NZ - 1, 0), (NZ - 1, 1))[index]
        return remote(rim, rim, rsend.at[index], rrecv, head=((z + by) % NZ) * 2 + column)

    @pl.when(is_root)
    def _():
        for group in range(4):
            from_root(group).start()

    own = pltpu.make_async_copy(raw, out.at[z, own_rows], lsem)
    own.start()
    for far in range(1, 9):
        for side in range(2):
            slot = slot_of(side, far)
            hop(side, far, slot).wait_recv()
            if far + 2 <= 8:
                go(hop(side, far + 2, slot))
            if far < 8:
                go(across(far + 8 * side, slot))
        if far == 6:

            @pl.when(is_relay)
            def _():
                from_root(0).wait_recv()
                for index in range(7):
                    from_relay(index).start()

    go(across(8, slot_of(0, 8)))
    for index in range(16):
        slot = slot_of(0, index) if index <= 8 else slot_of(1, index - 8)
        landed = out.at[slot, mate_rows]
        remote(landed, landed, ysend.at[index], yrecv.at[index], head=mate).wait_recv()
    own.wait()

    @pl.when(jnp.logical_not(is_relay))
    def _():
        from_root(0).wait_recv()

    @pl.when(is_relay)
    def _():
        for index in range(7):
            from_relay(index).wait_send()

    @pl.when(is_root)
    def _():
        for group in range(4):
            from_root(group).wait_send()

    for copy in sent:
        copy.wait_send()


def gather(raw):
    rows, width = raw.shape
    dma = pltpu.SemaphoreType.DMA
    return pl.pallas_call(
        gather_kernel,
        out_shape=(
            jax.ShapeDtypeStruct((NZ, 2 * rows, width), raw.dtype),
            jax.ShapeDtypeStruct((16, width), raw.dtype),
        ),
        in_specs=[VMEM_SPEC],
        out_specs=(VMEM_SPEC, VMEM_SPEC),
        scratch_shapes=[
            dma((2, 9)),
            dma((2, 9)),
            dma((16,)),
            dma((16,)),
            dma,
            dma((4,)),
            dma((7,)),
            dma,
        ],
        compiler_params=pltpu.CompilerParams(
            collective_id=0, has_side_effects=True, vmem_limit_bytes=8 * 1024 * 1024
        ),
        name="gather_bc",
    )(raw)


def split(value):
    high = value.astype(BF16)
    return high, (value - high.astype(F32)).astype(BF16)


def dot(a, b, ca, cb):
    return lax.dot_general(a, b, (((ca,), (cb,)), ((), ())), preferred_element_type=F32)


def spread_heads(column):
    rows = column.shape[0]
    return jnp.concatenate(
        [jnp.broadcast_to(column[:, h : h + 1], (rows, HEAD_DIM)) for h in range(4)], axis=1
    )


def lane_row(tile):
    return jnp.concatenate([tile[h : h + 1, :] for h in range(4)], axis=1)


def mixer_kernel(
    raw,
    rim,
    small,
    dt,
    x_far,
    z_far,
    out,
    x_ref,
    z_ref,
    act,
    padded,
    cums,
    offsets,
    starts,
    priors,
    state,
    total,
    mixed,
    message,
    fade,
    landed,
    fades,
    prefix,
    entry,
    squares,
    pair,
    parts,
    local_sem,
    fsend,
    frecv,
    asend,
    arecv,
    bsend,
    brecv,
    psend,
    precv,
    zsend,
    zrecv,
):
    seq = lax.axis_index("seq")
    head = lax.axis_index("head")
    z = head // 2
    yl = head % 2
    mate = z * 2 + 1 - yl
    blocks = x_ref.shape[0] // BLOCK
    others = [(seq + hop) % NSEQ for hop in (10, 6, 14, 11, 9, 5, 13, 7, 15, 3, 8, 12, 4, 2, 1)]
    hops = (8, 7, 9, 6, 10, 5, 11, 4, 12, 3, 13, 2, 14, 1, 15)
    places = [(z + hop) % NZ for hop in hops]
    targets = [{"seq": other} for other in others] + [{"head": mate}]
    targets = targets + [{"head": place * 2 + yl} for place in places]
    barrier = pltpu.get_barrier_semaphore()
    for where in targets:
        pl.semaphore_signal(
            barrier, inc=1, device_id=where, device_id_type=pl.DeviceIdType.MESH
        )
    fetch_x = pltpu.make_async_copy(x_far, x_ref, local_sem.at[0])
    fetch_z = pltpu.make_async_copy(z_far, z_ref, local_sem.at[1])
    fetch_x.start()
    fetch_z.start()

    def rows_of(block):
        return pl.ds(pl.multiple_of(block * BLOCK, BLOCK), BLOCK)

    rate = small[8:16, 0:BLOCK]
    row = lax.broadcasted_iota(jnp.int32, (BLOCK, BLOCK), 0)
    column = lax.broadcasted_iota(jnp.int32, (BLOCK, BLOCK), 1)
    upper = jnp.where(row <= column, 1.0, 0.0).astype(BF16)
    padded[0:8, :] = jnp.where(seq == 0, 0.0, rim[...].astype(F32)[8:16, :])
    state[...] = jnp.zeros_like(state)
    total[...] = jnp.zeros_like(total)
    squares[...] = jnp.zeros_like(squares)
    fetch_x.wait()

    def first_pass(block, _):
        rows = rows_of(block)
        padded[8 : 8 + BLOCK, :] = raw[rows, :].astype(F32)
        summed = jnp.broadcast_to(small[4:5, :], (BLOCK, 2 * STATE))
        for tap in range(4):
            summed = summed + small[tap : tap + 1, :] * padded[5 + tap : 5 + tap + BLOCK, :]
        acted = jax.nn.silu(summed).astype(BF16)
        act[rows, :] = acted
        padded[0:8, :] = padded[BLOCK : BLOCK + 8, :]
        raw_dt = dt[block]
        size = jnp.maximum(raw_dt, 0.0) + jnp.log1p(jnp.exp(-jnp.abs(raw_dt)))
        log_step = rate * size
        high = log_step.astype(BF16)
        middle, low = split(log_step - high.astype(F32))
        cum = (dot(low, upper, 1, 0) + dot(middle, upper, 1, 0)) + dot(high, upper, 1, 0)
        offset = cum - jnp.log(size)
        cums[block] = cum
        offsets[block] = offset
        last = cum[:, BLOCK - 1 : BLOCK]
        tail = jnp.exp(jnp.transpose(last - offset))
        high, low = split(x_ref[rows, :].astype(F32) * spread_heads(tail))
        b_in = acted[:, :STATE]
        ends = jnp.broadcast_to(last, (8, 128))
        starts[block] = state[...]
        priors[block] = jnp.exp(total[...])
        fresh = dot(b_in, high, 0, 0) + dot(b_in, low, 0, 0)
        state[...] = lane_row(jnp.exp(ends)) * state[...] + fresh
        total[...] = total[...] + ends
        return 0

    lax.fori_loop(0, blocks, first_pass, 0)
    for k in range(NSEQ):
        message[k] = state[16 * k : 16 * k + 16, :].astype(BF16)
    fade[...] = jnp.exp(total[...])
    pl.semaphore_wait(barrier, len(targets))
    sent = []
    for other in others:
        copy = remote(fade, fades.at[seq], fsend.at[other], frecv.at[seq], seq=other)
        copy.start()
        sent.append(copy)
        copy = remote(message.at[other], landed.at[seq], asend.at[other], arecv.at[seq], seq=other)
        copy.start()
        sent.append(copy)
    landed[seq] = message[seq]
    fades[seq] = fade[...]

    causal = row >= column

    def inner_pass(block, _):
        rows = rows_of(block)
        gram = dot(act[rows, STATE:], act[rows, :STATE], 1, 1)
        at_all = jnp.transpose(cums[block])
        offset = offsets[block]
        for h in range(4):
            lanes = slice(h * HEAD_DIM, (h + 1) * HEAD_DIM)
            gap = at_all[:, h : h + 1] - offset[h : h + 1, :]
            decay = jnp.exp(jnp.where(causal, gap, -1e30))
            x_head = x_ref[rows, lanes]
            mixed[rows, lanes] = dot(
                (gram * decay).astype(BF16), x_head, 1, 0
            ) + small[6:7, lanes] * x_head.astype(F32)
        return 0

    lax.fori_loop(0, blocks // 2, inner_pass, 0)
    for other in others:
        remote(fades.at[other], fades.at[other], fsend.at[other], frecv.at[other], seq=other).wait_recv()
        remote(
            landed.at[other], landed.at[other], asend.at[other], arecv.at[other], seq=other
        ).wait_recv()
    running = jnp.zeros((16, x_ref.shape[1]), F32)
    for s in range(NSEQ):
        prefix[s] = running.astype(BF16)
        if s < NSEQ - 1:
            running = lane_row(fades[s]) * running + landed[s].astype(F32)
    for other in others:
        copy = remote(prefix.at[other], entry.at[seq], bsend.at[other], brecv.at[seq], seq=other)
        copy.start()
        sent.append(copy)
    entry[seq] = prefix[seq]
    lax.fori_loop(blocks // 2, blocks, inner_pass, 0)
    fetch_z.wait()
    for other in others:
        remote(
            entry.at[other], entry.at[other], bsend.at[other], brecv.at[other], seq=other
        ).wait_recv()
    state[...] = entry[...].astype(F32).reshape(state.shape)
    ones = jnp.ones((8, x_ref.shape[1]), BF16)

    def last_pass(block, _):
        rows = rows_of(block)
        high, low = split(starts[block] + lane_row(priors[block]) * state[...])
        c_out = act[rows, STATE:]
        carried = dot(c_out, high, 1, 0) + dot(c_out, low, 1, 0)
        scale = spread_heads(jnp.exp(jnp.transpose(cums[block])))
        gate = jax.nn.silu(z_ref[rows, :].astype(F32))
        gated = (mixed[rows, :] + scale * carried) * gate
        mixed[rows, :] = gated
        sums = dot(ones, (gated * gated).astype(BF16), 1, 1)
        squares[pl.ds(2 * block, 1), :] = sums[0:1, 0:128]
        squares[pl.ds(2 * block + 1, 1), :] = sums[0:1, 128:256]
        return 0

    lax.fori_loop(0, blocks, last_pass, 0)
    first = remote(squares, pair, psend, precv, head=mate)
    first.start()
    first.wait()
    parts[z] = squares[...] + pair[...]
    for place in places:
        copy = remote(
            parts.at[z], parts.at[z], zsend.at[place], zrecv.at[z], head=place * 2 + yl
        )
        copy.start()
        sent.append(copy)
    for place in reversed(places):
        remote(
            parts.at[place], parts.at[place], zsend.at[place], zrecv.at[place], head=place * 2 + yl
        ).wait_recv()
    whole = parts[0]
    for k in range(1, NZ):
        whole = whole + parts[k]
    pair[...] = lax.rsqrt(whole / INNER + 1e-05)

    def norm_pass(part, _):
        rows = pl.ds(pl.multiple_of(part * 128, 128), 128)
        inverse = jnp.transpose(jnp.broadcast_to(pair[pl.ds(part, 1), :], (8, 128)))[:, 0:1]
        out[rows, :] = (mixed[rows, :] * inverse * small[5:6, :]).astype(BF16)
        return 0

    lax.fori_loop(0, 2 * blocks, norm_pass, 0)
    for copy in sent:
        copy.wait_send()


def mixer(raw, rim, small, dt, x, z_gate):
    length, width = x.shape
    blocks = length // BLOCK
    far = pl.BlockSpec(memory_space=pl.ANY)
    dma = pltpu.SemaphoreType.DMA
    return pl.pallas_call(
        mixer_kernel,
        out_shape=jax.ShapeDtypeStruct((length, width), BF16),
        in_specs=[VMEM_SPEC] * 4 + [far, far],
        out_specs=VMEM_SPEC,
        scratch_shapes=[
            pltpu.VMEM((length, width), BF16),
            pltpu.VMEM((length, width), BF16),
            pltpu.VMEM((length, 2 * STATE), BF16),
            pltpu.VMEM((BLOCK + 8, 2 * STATE), F32),
            pltpu.VMEM((blocks, 8, BLOCK), F32),
            pltpu.VMEM((blocks, 8, BLOCK), F32),
            pltpu.VMEM((blocks, STATE, width), F32),
            pltpu.VMEM((blocks, 8, 128), F32),
            pltpu.VMEM((STATE, width), F32),
            pltpu.VMEM((8, 128), F32),
            pltpu.VMEM((length, width), F32),
            pltpu.VMEM((NSEQ, 16, width), BF16),
            pltpu.VMEM((8, 128), F32),
            pltpu.VMEM((NSEQ, 16, width), BF16),
            pltpu.VMEM((NSEQ, 8, 128), F32),
            pltpu.VMEM((NSEQ, 16, width), BF16),
            pltpu.VMEM((NSEQ, 16, width), BF16),
            pltpu.VMEM((16, 128), F32),
            pltpu.VMEM((16, 128), F32),
            pltpu.VMEM((NZ, 16, 128), F32),
            dma((2,)),
        ]
        + [dma((NSEQ,))] * 6
        + [dma, dma, dma((NZ,)), dma((NZ,))],
        compiler_params=pltpu.CompilerParams(
            collective_id=1, has_side_effects=True, vmem_limit_bytes=48 * 1024 * 1024
        ),
        name="mixer",
    )(raw, rim, small, dt, x, z_gate)


def on_device(x_inner, z_gate, bc_raw, conv_weight, conv_bias, dt_raw, a_log, d_skip, norm_gain):
    length = x_inner.shape[0]
    dt = jnp.pad(dt_raw.T, ((0, 4), (0, 0)))
    dt = jnp.transpose(dt.reshape(8, length // BLOCK, BLOCK), (1, 0, 2))
    width = 2 * STATE
    small = jnp.concatenate(
        [
            conv_weight,
            conv_bias[None, :],
            norm_gain[None, :],
            jnp.repeat(d_skip, HEAD_DIM)[None, :],
            jnp.zeros((1, width), F32),
            jnp.broadcast_to(jnp.pad(-jnp.exp(a_log), (0, 4))[:, None], (8, width)),
        ],
        axis=0,
    )
    gathered, rim = gather(bc_raw)
    raw = gathered.reshape(length, 2 * STATE)
    return mixer(raw, rim, small, dt, x_inner, z_gate)


def solution(mesh):
    placed = (
        P("seq", "head"),
        P("seq", "head"),
        P(("seq", "head"), None),
        P(),
        P(),
        P("seq", "head"),
        P("head"),
        P("head"),
        P("head"),
    )
    return jax.shard_map(
        on_device, mesh=mesh, in_specs=placed, out_specs=P("seq", "head"), check_vma=False
    )
```
